256 devices in a mesh: member: 8 (over x_hi, y), lat: 16 (over z, core), lon: 2 (over x_lo).
Axes of the slice: x: 4 (x_hi: 2, x_lo: 2; x = x_hi * 2 + x_lo), y: 4, z: 8, core: 2. Of those that a mesh axis runs over, the one named last changes fastest.
Arguments:
- state: bfloat16 [72, 128, 256], P(None, 'lat', 'lon'), may hold values from -6 to 6
- noise: bfloat16 [8, 2, 8, 128, 256], P('member', None, None, 'lat', 'lon'), may hold values from -6 to 6
- target: bfloat16 [2, 72, 128, 256], P(None, None, 'lat', 'lon'), may hold values from -6 to 6
- encoder_state_weight: bfloat16 [512, 72], replicated, may hold values from -0.75 to 0.75
- enc_noise: bfloat16 [512, 8], replicated, may hold values from -2 to 2
- lat_taps: float32 [4, 7, 512], replicated, may hold values from -1.75 to 1.75
- lon_taps: float32 [4, 6, 512], replicated, may hold values from -1.75 to 1.75
- gains: float32 [4, 512], replicated, may hold values from 0.25 to 1.75
- mix: bfloat16 [4, 512, 512], replicated, may hold values from -0.25 to 0.25
- decode: bfloat16 [72, 512], replicated, may hold values from -0.25 to 0.25
Outputs:
- trajectory_predictions: bfloat16 [8, 2, 72, 128, 256], P('member', None, None, 'lat', 'lon')
- probabilistic_error: float32 [72, 128, 256], P('member', 'lat', 'lon')
The draws below stay inside these ranges and needn't reach their ends.
All inputs are finite; a program needn't handle non-finite values.
Results may differ from the reference program's by a relative error of at most 0.015.
Values may be sent and summed in bfloat16 or wider, within the bound.
No kernel may reach another device: no remote copies, remote signals or barrier semaphores. Data moves between devices by JAX's collectives and lax.ppermute only.
A program may use at most 64 MiB of HBM per device.

```python
import jax
import jax.numpy as jnp
from jax import lax

C = 512
VAR = 72
NOISE = 8
LAYERS = 4
STEPS = 2
MEMBERS = 8
NLAT = 128
NLON = 256


def block_scale(own_key, shape, pieces, low, top_value):
    def one(position, blocks):
        steps = jax.random.uniform(jax.random.fold_in(jax.random.fold_in(own_key, 6), position), (blocks,), jnp.float32, low / len(pieces), top_value / len(pieces))
        return jnp.repeat(jnp.exp(steps), shape[position] // blocks).reshape((-1,) + (1,) * (len(shape) - position - 1))

    level = one(*pieces[0])
    for cut in pieces[1:]:
        level = level * one(*cut)
    return level


def gaussian(own_key, extent, scale, limit, shards=(), dtype=jnp.bfloat16):
    level = block_scale(own_key, extent, shards, -0.22, 0.18) if shards else 1.0
    entries = jax.random.normal(own_key, extent, jnp.float32) * scale * level
    return jnp.minimum(jnp.maximum(entries, -limit), limit).astype(dtype)


def setup_inputs(seed: int = 0) -> dict:
    streams_of = jax.random.split(jax.random.key(seed), 11)
    return {
        "state": gaussian(streams_of[0], (VAR, NLAT, NLON), 1.0, 6.0, ((1, 16), (2, 2))),
        "noise": gaussian(streams_of[1], (MEMBERS, STEPS, NOISE, NLAT, NLON), 1.0, 6.0, ((0, 8), (3, 16), (4, 2))),
        "target": gaussian(streams_of[2], (STEPS, VAR, NLAT, NLON), 1.0, 6.0, ((2, 16), (3, 2))),
        "encoder_state_weight": gaussian(streams_of[3], (C, VAR), VAR ** -0.5, 0.75),
        "enc_noise": gaussian(streams_of[4], (C, NOISE), NOISE ** -0.5, 2.0),
        "lat_taps": gaussian(streams_of[5], (LAYERS, 7, C), 13 ** -0.5, 1.75, (), jnp.float32),
        "lon_taps": gaussian(streams_of[6], (LAYERS, 6, C), 13 ** -0.5, 1.75, (), jnp.float32),
        "gains": jnp.clip(1.0 + 0.15 * jax.random.normal(streams_of[7], (LAYERS, C), jnp.float32), 0.25, 1.75),
        "mix": gaussian(streams_of[8], (LAYERS, C, C), C ** -0.5, 0.25),
        "decode": gaussian(streams_of[9], (VAR, C), C ** -0.5, 0.25),
    }


epsilon = 1e-05

def convolve(hidden, lat_row, lon_row):
    height = hidden.shape[1]
    width = hidden.shape[2]
    lat_pad = jnp.pad(hidden, ((0, 0), (3, 3), (0, 0)))
    lon_pad = jnp.concatenate([hidden[:, :, width - 3:], hidden, hidden[:, :, :3]], axis=2)
    total = jnp.zeros(hidden.shape, jnp.float32)
    for offset in range(7):
        total = total + lat_row[offset][:, None, None] * lat_pad[:, offset:offset + height, :].astype(jnp.float32)
    for column, offset in enumerate([0, 1, 2, 4, 5, 6]):
        total = total + lon_row[column][:, None, None] * lon_pad[:, :, offset:offset + width].astype(jnp.float32)
    return total

def layer_step(hidden, lat_row, lon_row, gain_row, matrix):
    conv = convolve(hidden, lat_row, lon_row)
    center = lax.optimization_barrier(jnp.mean(conv, axis=0))
    variance = lax.optimization_barrier(jnp.mean(jnp.square(conv - center), axis=0))
    normalized_fields = ((conv - center) * lax.rsqrt(variance + epsilon) * gain_row[:, None, None]).astype(jnp.bfloat16)
    channel_list = hidden.shape[0]
    mixed = jnp.dot(matrix, normalized_fields.reshape(channel_list, -1), preferred_element_type=jnp.float32).reshape(hidden.shape)
    return (hidden.astype(jnp.float32) + jax.nn.gelu(mixed, approximate=True)).astype(jnp.bfloat16)

def reference(state, noise, target, encoder_state_weight, enc_noise, lat_taps, lon_taps, gains, mix, decode):
    members = noise.shape[0]
    step_count = noise.shape[1]
    layer_count = mix.shape[0]
    channel_list = mix.shape[1]
    quantity_total, height, width = state.shape
    noise_count = noise.shape[2]
    whole_ensemble_grids = []
    for member_id in range(members):
        current = state
        increment_errors = []
        for step in range(step_count):
            hidden = jnp.dot(encoder_state_weight, current.reshape(quantity_total, -1), preferred_element_type=jnp.float32) + jnp.dot(enc_noise, noise[member_id, step].reshape(noise_count, -1), preferred_element_type=jnp.float32)
            hidden = hidden.reshape(channel_list, height, width).astype(jnp.bfloat16)
            for level in range(layer_count):
                hidden = layer_step(hidden, lat_taps[level], lon_taps[level], gains[level], mix[level])
            decoded = jnp.dot(decode, hidden.reshape(channel_list, -1), preferred_element_type=jnp.float32).reshape(quantity_total, height, width)
            current = (current.astype(jnp.float32) + decoded).astype(jnp.bfloat16)
            increment_errors.append(current)
        whole_ensemble_grids.append(jnp.stack(increment_errors))
    trajectory_predictions = jnp.stack(whole_ensemble_grids)
    quantities_real = trajectory_predictions.astype(jnp.float32)
    skill = lax.optimization_barrier(jnp.sum(jnp.abs(quantities_real - target.astype(jnp.float32)[None]), axis=(0, 1)))
    spread = jnp.zeros((quantity_total, height, width), jnp.float32)
    for other in range(members):
        spread = spread + lax.optimization_barrier(jnp.sum(jnp.abs(quantities_real - quantities_real[other][None]), axis=(0, 1)))
    scale = float(members)
    probabilistic_error = skill / scale - spread / (2.0 * scale * (scale - 1.0))
    return (trajectory_predictions, probabilistic_error)
```

```python
import functools

import jax
import jax.numpy as jnp
from jax import lax
from jax.experimental import pallas as pl
from jax.experimental.pallas import tpu as pltpu
from jax.sharding import PartitionSpec as P

epsilon = 1e-05
REACH = 3
F32 = jnp.float32
BF16 = jnp.bfloat16


def step_kernel(
    layers,
    variables,
    carry_noise,
    up_ref,
    own_ref,
    down_ref,
    enc_ref,
    taps_ref,
    mix_ref,
    dec_ref,
    out_ref,
    h_ref,
    v_ref,
    acc_ref,
):
    halo = up_ref.shape[0]
    own = own_ref.shape[0]
    channels = h_ref.shape[1]
    lanes = h_ref.shape[2]
    inputs = enc_ref.shape[1]
    group = 16
    blocks = channels // group
    band = lax.axis_index("lat") // 2
    first = band * own - halo
    height = (lax.axis_size("lat") // 2) * own

    enc = enc_ref[...]

    def encode(source, offset):
        def pair(k, _):
            x = jnp.concatenate([source[2 * k, :inputs], source[2 * k + 1, :inputs]], axis=1)
            y = jnp.dot(enc, x, preferred_element_type=F32).astype(BF16)
            h_ref[offset + 2 * k] = y[:, :lanes]
            h_ref[offset + 2 * k + 1] = y[:, lanes:]
            return 0

        lax.fori_loop(0, source.shape[0] // 2, pair, 0)

    encode(up_ref, 0)
    encode(own_ref, halo)
    encode(down_ref, halo + own)

    c0 = 2.0 * 0.7978845608028654
    c1 = 8.0 * 0.7978845608028654 * 0.044715

    def layer(level, _):
        out_rows = own + 2 * halo - 2 * REACH * (level + 1)

        def pair(k, _):
            k = 2 * k
            sums = [jnp.zeros((group, lanes), F32) for _ in range(4)]
            for part in range(blocks // 4):
                small = [None] * 4
                for sub in range(4):
                    b = part * 4 + sub
                    span = pl.ds(b * group, group)
                    rows = [h_ref[k + i, span, :] for i in range(8)]
                    for r in range(2):
                        mid = rows[r + REACH]
                        total = None
                        for d in range(7):
                            term = taps_ref[level, d, span, :] * rows[r + d]
                            total = term if total is None else total + term
                        for column, d in enumerate([-3, -2, -1, 1, 2, 3]):
                            total = total + taps_ref[level, 7 + column, span, :] * pltpu.roll(
                                mid, (-d) % lanes, 1
                            )
                        v_ref[span, pl.ds(r * lanes, lanes)] = total
                        square = total * total
                        small[r] = total if small[r] is None else small[r] + total
                        small[2 + r] = square if small[2 + r] is None else small[2 + r] + square
                for i in range(4):
                    sums[i] = sums[i] + small[i].astype(F32)
            scales = []
            for r in range(2):
                mean = jnp.sum(sums[r], axis=0, keepdims=True) * (1.0 / channels)
                second = jnp.sum(sums[2 + r], axis=0, keepdims=True) * (1.0 / channels)
                variance = jnp.maximum(second - mean * mean, 0.0)
                row = first + REACH * (level + 1) + k + r
                inside = jnp.logical_and(row >= 0, row < height)
                scales.append(jnp.where(inside, 0.5 * lax.rsqrt(variance + epsilon), 0.0))
            scale = jnp.concatenate(scales, axis=1)
            acc_ref[...] = jnp.dot(mix_ref[level], v_ref[...], preferred_element_type=F32)
            for b in range(blocks):
                span = pl.ds(b * group, group)
                half = (acc_ref[span, :] * scale).astype(BF16)
                inner = half * (half * half * c1 + c0)
                gate = half + half * jnp.tanh(inner)
                for r in range(2):
                    h_ref[k + r, span, :] = (
                        h_ref[k + REACH + r, span, :] + gate[:, r * lanes : (r + 1) * lanes]
                    )
            return 0

        lax.fori_loop(0, out_rows // 2, pair, 0)
        return 0

    lax.fori_loop(0, layers, layer, 0)

    dec = dec_ref[...]

    def decode(k, _):
        h = jnp.concatenate([h_ref[2 * k], h_ref[2 * k + 1]], axis=1)
        y = jnp.dot(dec, h, preferred_element_type=F32)
        for r in range(2):
            row = 2 * k + r
            base = own_ref[row, :variables].astype(F32)
            out_ref[row, :variables] = (base + y[:, r * lanes : (r + 1) * lanes]).astype(BF16)
            if carry_noise:
                out_ref[row, variables:] = own_ref[row, inputs:]
        return 0

    lax.fori_loop(0, own // 2, decode, 0)


def rollout_step(up, own, down, enc, taps, mix, dec, carry_noise):
    layers, channels = mix.shape[0], mix.shape[1]
    variables = dec.shape[0]
    rows, lanes = own.shape[0], own.shape[2]
    total = rows + 2 * up.shape[0]
    out_channels = enc.shape[1] if carry_noise else variables
    return pl.pallas_call(
        functools.partial(step_kernel, layers, variables, carry_noise),
        out_shape=jax.ShapeDtypeStruct((rows, out_channels, lanes), BF16),
        in_specs=[pl.BlockSpec(memory_space=pltpu.VMEM)] * 7,
        out_specs=pl.BlockSpec(memory_space=pltpu.VMEM),
        scratch_shapes=[
            pltpu.VMEM((total, channels, lanes), BF16),
            pltpu.VMEM((channels, 2 * lanes), BF16),
            pltpu.VMEM((channels, 2 * lanes), F32),
        ],
        compiler_params=pltpu.CompilerParams(vmem_limit_bytes=48 * 1024 * 1024),
        name="rollout_step",
    )(up, own, down, enc, taps, mix, dec)


def z_shift(block, reach, bands):
    pairs = [(i, i + reach) for i in range(bands) if 0 <= i + reach < bands]
    return lax.ppermute(block, "lat", pairs)


def local(
    state, noise, target, encoder_state_weight, enc_noise, lat_taps, lon_taps, gains, mix, decode
):
    variables, rows_dev, cols_dev = state.shape
    layers, channels = mix.shape[0], mix.shape[1]
    noise_count = noise.shape[2]
    inputs = variables + noise_count
    bands = lax.axis_size("lat")
    halo = REACH * layers
    side = 2 * halo
    core = lax.axis_index("lat") % 2
    sibling = [(i, i ^ 1) for i in range(bands)]

    gathered = jnp.concatenate([state, noise[0, 0], noise[0, 1]], axis=0)
    mine = jnp.transpose(gathered, (1, 0, 2))
    other = lax.ppermute(mine, "lat", sibling)
    low = jnp.where(core == 0, mine, other)
    high = jnp.where(core == 0, other, mine)
    block = jnp.concatenate([low, high], axis=0)
    rows = block.shape[0]
    right = block[:, :, cols_dev - side :]
    left = block[:, :, :side]
    edge = jnp.where(core == 0, right, left).reshape(4, rows // 4, -1, side)
    packed = jnp.concatenate([edge[i] for i in range(4)], axis=-1)
    packed = lax.ppermute(packed, "lon", [(0, 1), (1, 0)])
    edge = jnp.concatenate([packed[:, :, i * side : (i + 1) * side] for i in range(4)], axis=0)
    block = jnp.concatenate(
        [
            jnp.where(core == 1, edge, left),
            block[:, :, side : cols_dev - side],
            jnp.where(core == 0, edge, right),
        ],
        axis=-1,
    )
    up = z_shift(block[rows - halo :, :inputs], 2, bands)
    down = z_shift(block[:halo, :inputs], -2, bands)

    enc = jnp.concatenate([encoder_state_weight, enc_noise], axis=1)
    taps = jnp.concatenate([lat_taps, lon_taps], axis=1).astype(BF16)
    taps = jnp.broadcast_to(taps[..., None], taps.shape + (cols_dev,))
    scaled = mix.astype(F32) * gains[:, None, :]
    scaled = (scaled - jnp.mean(scaled, axis=2, keepdims=True)).astype(BF16)

    first = rollout_step(up, block, down, enc, taps, scaled, decode, True)
    up = z_shift(first[rows - halo :], 2, bands)
    down = z_shift(first[:halo], -2, bands)
    second = rollout_step(up, first, down, enc, taps, scaled, decode, False)

    both = jnp.stack([first[:, :variables], second])
    lower = both[:, :rows_dev]
    upper = both[:, rows_dev:]
    kept = jnp.where(core == 0, lower, upper)
    sent = jnp.where(core == 0, upper, lower)
    taken = lax.ppermute(sent, "lat", sibling)
    lane = lax.broadcasted_iota(jnp.int32, kept.shape, 3)
    keep = (lane >= cols_dev // 2) == (core == 1)
    merged = jnp.where(keep, kept, taken)
    trajectory_predictions = jnp.transpose(merged, (0, 2, 1, 3))[None]

    members = lax.axis_size("member")
    scale = float(members)
    regrouped = lax.all_to_all(
        trajectory_predictions, "member", split_axis=2, concat_axis=0, tiled=True
    )
    quantities_real = regrouped.astype(F32)
    part = variables // members
    start = lax.axis_index("member") * part
    target_block = lax.dynamic_slice_in_dim(target, start, part, 1).astype(F32)
    skill = jnp.sum(jnp.abs(quantities_real - target_block[None]), axis=(0, 1))
    spread = jnp.zeros(skill.shape, F32)
    for i in range(members):
        for j in range(i):
            spread = spread + jnp.sum(jnp.abs(quantities_real[i] - quantities_real[j]), axis=0)
    probabilistic_error = skill / scale - spread / (scale * (scale - 1.0))
    return (trajectory_predictions, probabilistic_error)


def solution(mesh):
    in_specs = (
        P(None, "lat", "lon"),
        P("member", None, None, "lat", "lon"),
        P(None, None, "lat", "lon"),
        P(),
        P(),
        P(),
        P(),
        P(),
        P(),
        P(),
    )
    out_specs = (P("member", None, None, "lat", "lon"), P("member", "lat", "lon"))
    return jax.shard_map(local, mesh=mesh, in_specs=in_specs, out_specs=out_specs, check_vma=False)
```

```python
import functools

import jax
import jax.numpy as jnp
from jax import lax
from jax.experimental import pallas as pl
from jax.experimental.pallas import tpu as pltpu
from jax.sharding import PartitionSpec as P

epsilon = 1e-05
REACH = 3
F32 = jnp.float32
BF16 = jnp.bfloat16


def step_kernel(
    width,
    up_ref,
    own_ref,
    down_ref,
    enc_ref,
    taps_ref,
    mix_ref,
    dec_ref,
    out_ref,
    h_ref,
    v_ref,
    acc_ref,
    scale_ref,
):
    halo = up_ref.shape[0]
    own = own_ref.shape[0]
    planes, _, _, lanes = h_ref.shape
    span = own_ref.shape[2]
    channels = planes * lanes
    inputs = enc_ref.shape[0]
    layers = mix_ref.shape[0]
    variables = dec_ref.shape[0]
    position = lax.axis_index("lat")
    band = position // 2
    first = band * own - halo
    height = (lax.axis_size("lat") // 2) * own
    margin = (width - span // 2) // 2
    inset = -margin % 8
    start = jnp.where(
        position % 2 == 0, span - margin - inset, span // 2 - margin - inset
    )

    def encode(source, offset):
        def one(k, _):
            y = lax.dot_general(
                source[k, :inputs],
                enc_ref[...],
                (((0,), (0,)), ((), ())),
                preferred_element_type=F32,
            )
            for chunk in range(span // 8):
                place = pl.multiple_of(8 + lax.rem(8 * chunk - start + span, span), 8)
                for t in range(planes):
                    h_ref[t, offset + k, pl.ds(place, 8), :] = y[
                        8 * chunk : 8 * chunk + 8, t * lanes : (t + 1) * lanes
                    ]
            return 0

        lax.fori_loop(0, source.shape[0], one, 0)

    encode(up_ref, 0)
    encode(own_ref, halo)
    encode(down_ref, halo + own)

    c0 = 2.0 * 0.7978845608028654
    c1 = 8.0 * 0.7978845608028654 * 0.044715

    for level in range(layers):
        edge = REACH * (level + 1)
        left = (inset + edge) // 8 * 8
        tiles = -(-(inset + width - edge - left) // 16)
        groups = -(-(own + 2 * halo - 2 * edge) // 4)

        def group(g, _, level=level, edge=edge, tiles=tiles, left=left + 8):
            k = 4 * g

            def convolve(j, _):
                c = pl.multiple_of(left + 16 * j, 8)
                for t in range(planes):
                    part = slice(t * lanes, (t + 1) * lanes)
                    rows = [h_ref[t, k + i, pl.ds(c, 16), :].astype(BF16) for i in range(10)]
                    totals = [None] * 4
                    for d in range(7):
                        tap = taps_ref[level, d, :, part]
                        for r in range(4):
                            term = rows[r + d] * tap
                            totals[r] = term if d == 0 else totals[r] + term
                    for column, d in enumerate([-3, -2, -1, 1, 2, 3]):
                        tap = taps_ref[level, 7 + column, :, part]
                        for r in range(4):
                            shifted = h_ref[t, k + r + REACH, pl.ds(c + d, 16), :].astype(BF16)
                            totals[r] = totals[r] + shifted * tap
                    for r in range(4):
                        m = pl.multiple_of(r * 16 * tiles + 16 * j, 16)
                        v_ref[pl.ds(m, 16), part] = totals[r]
                return 0

            lax.fori_loop(0, tiles, convolve, 0)
            size = 64 * tiles
            acc_ref[:size] = jnp.dot(
                v_ref[:size], mix_ref[level], preferred_element_type=F32
            )
            for r in range(4):
                row = first + edge + k + r
                inside = jnp.logical_and(row >= 0, row < height).astype(F32)
                for j in range(tiles):
                    m = r * 16 * tiles + 16 * j
                    parts = [
                        v_ref[m : m + 16, t * lanes : (t + 1) * lanes] for t in range(planes)
                    ]
                    total = functools.reduce(jnp.add, parts).astype(F32)
                    square = functools.reduce(jnp.add, [x * x for x in parts]).astype(F32)
                    mean = jnp.sum(total, axis=1, keepdims=True)
                    second = jnp.sum(square, axis=1, keepdims=True)
                    variance = jnp.maximum(
                        second * (1.0 / channels) - mean * mean * (1.0 / channels**2), 0.0
                    )
                    scale = lax.rsqrt(variance + epsilon) * inside
                    scale_ref[m : m + 16, :] = jnp.broadcast_to(scale, (16, lanes))
            for j in range(tiles):
                c = left + 16 * j
                for r in range(4):
                    m = r * 16 * tiles + 16 * j
                    scale = scale_ref[m : m + 16, :].astype(BF16)
                    for t in range(planes):
                        part = slice(t * lanes, (t + 1) * lanes)
                        half = acc_ref[m : m + 16, part].astype(BF16) * scale
                        inner = half * (half * half * c1 + c0)
                        gate = half + half * jnp.tanh(inner)
                        h_ref[t, k + r, c : c + 16, :] = h_ref[
                            t, k + REACH + r, c : c + 16, :
                        ] + gate.astype(F32)
            return 0

        lax.fori_loop(0, groups, group, 0)

    def decode(k, _):
        h = jnp.concatenate([h_ref[t, k, pl.ds(8, span), :] for t in range(planes)], axis=1).astype(BF16)
        y = lax.dot_general(
            dec_ref[...], h, (((1,), (1,)), ((), ())), preferred_element_type=F32
        )
        y = pltpu.roll(y, start, 1)
        out_ref[k, :variables] = (own_ref[k, :variables].astype(F32) + y).astype(BF16)
        if out_ref.shape[1] > variables:
            out_ref[k, variables:] = own_ref[k, inputs:]
        return 0

    lax.fori_loop(0, own, decode, 0)


def rollout_step(up, own, down, enc, taps, mix, dec, width, carry_noise):
    channels = mix.shape[1]
    variables = dec.shape[0]
    rows, lanes = own.shape[0], own.shape[2]
    total = rows + 2 * up.shape[0] + 4
    cells = 64 * (-(-(width - 2 * REACH) // 16))
    out_channels = enc.shape[0] if carry_noise else variables
    return pl.pallas_call(
        functools.partial(step_kernel, width),
        out_shape=jax.ShapeDtypeStruct((rows, out_channels, lanes), BF16),
        in_specs=[pl.BlockSpec(memory_space=pltpu.VMEM)] * 7,
        out_specs=pl.BlockSpec(memory_space=pltpu.VMEM),
        scratch_shapes=[
            pltpu.VMEM((channels // lanes, total, lanes + 24, lanes), F32),
            pltpu.VMEM((cells, channels), BF16),
            pltpu.VMEM((cells, channels), F32),
            pltpu.VMEM((cells, lanes), F32),
        ],
        compiler_params=pltpu.CompilerParams(vmem_limit_bytes=48 * 1024 * 1024),
        name="rollout_step",
    )(up, own, down, enc, taps, mix, dec)


def z_shift(block, reach, bands):
    pairs = [(i, i + reach) for i in range(bands) if 0 <= i + reach < bands]
    return lax.ppermute(block, "lat", pairs)


def local(
    state, noise, target, encoder_state_weight, enc_noise, lat_taps, lon_taps, gains, mix, decode
):
    variables, rows_dev, cols_dev = state.shape
    layers, channels = mix.shape[0], mix.shape[1]
    noise_count = noise.shape[2]
    inputs = variables + noise_count
    bands = lax.axis_size("lat")
    halo = REACH * layers
    side = 2 * halo
    core = lax.axis_index("lat") % 2
    sibling = [(i, i ^ 1) for i in range(bands)]

    gathered = jnp.concatenate([state, noise[0, 0], noise[0, 1]], axis=0)
    mine = jnp.transpose(gathered, (1, 0, 2))
    other = lax.ppermute(mine, "lat", sibling)
    low = jnp.where(core == 0, mine, other)
    high = jnp.where(core == 0, other, mine)
    block = jnp.concatenate([low, high], axis=0)
    rows = block.shape[0]
    right = block[:, :, cols_dev - side :]
    left = block[:, :, :side]
    edge = jnp.where(core == 0, right, left).reshape(4, rows // 4, -1, side)
    packed = jnp.concatenate([edge[i] for i in range(4)], axis=-1)
    packed = lax.ppermute(packed, "lon", [(0, 1), (1, 0)])
    edge = jnp.concatenate([packed[:, :, i * side : (i + 1) * side] for i in range(4)], axis=0)
    block = jnp.concatenate(
        [
            jnp.where(core == 1, edge, left),
            block[:, :, side : cols_dev - side],
            jnp.where(core == 0, edge, right),
        ],
        axis=-1,
    )
    up = z_shift(block[rows - halo :, :inputs], 2, bands)
    down = z_shift(block[:halo, :inputs], -2, bands)

    enc = jnp.concatenate([encoder_state_weight, enc_noise], axis=1).T
    taps = jnp.concatenate([lat_taps, lon_taps], axis=1).astype(BF16)
    taps = jnp.broadcast_to(taps[:, :, None, :], taps.shape[:2] + (16, channels))
    scaled = mix.astype(F32) * (0.5 * gains[:, None, :])
    scaled = (scaled - jnp.mean(scaled, axis=2, keepdims=True)).astype(BF16)
    scaled = jnp.transpose(scaled, (0, 2, 1))

    first = rollout_step(up, block, down, enc, taps, scaled, decode, cols_dev // 2 + 2 * side, True)
    up = z_shift(first[rows - halo :], 2, bands)
    down = z_shift(first[:halo], -2, bands)
    second = rollout_step(up, first, down, enc, taps, scaled, decode, cols_dev // 2 + side, False)

    both = jnp.stack([first[:, :variables], second])
    lower = both[:, :rows_dev]
    upper = both[:, rows_dev:]
    kept = jnp.where(core == 0, lower, upper)
    sent = jnp.where(core == 0, upper, lower)
    taken = lax.ppermute(sent, "lat", sibling)
    lane = lax.broadcasted_iota(jnp.int32, kept.shape, 3)
    keep = (lane >= cols_dev // 2) == (core == 1)
    merged = jnp.where(keep, kept, taken)
    trajectory_predictions = jnp.transpose(merged, (0, 2, 1, 3))[None]

    members = lax.axis_size("member")
    scale = float(members)
    regrouped = lax.all_to_all(
        trajectory_predictions, "member", split_axis=2, concat_axis=0, tiled=True
    )
    quantities_real = regrouped.astype(F32)
    part = variables // members
    start = lax.axis_index("member") * part
    target_block = lax.dynamic_slice_in_dim(target, start, part, 1).astype(F32)
    skill = jnp.sum(jnp.abs(quantities_real - target_block[None]), axis=(0, 1))
    spread = jnp.zeros(skill.shape, F32)
    for i in range(members):
        for j in range(i):
            spread = spread + jnp.sum(jnp.abs(quantities_real[i] - quantities_real[j]), axis=0)
    probabilistic_error = skill / scale - spread / (scale * (scale - 1.0))
    return (trajectory_predictions, probabilistic_error)


def solution(mesh):
    in_specs = (
        P(None, "lat", "lon"),
        P("member", None, None, "lat", "lon"),
        P(None, None, "lat", "lon"),
        P(),
        P(),
        P(),
        P(),
        P(),
        P(),
        P(),
    )
    out_specs = (P("member", None, None, "lat", "lon"), P("member", "lat", "lon"))
    return jax.shard_map(local, mesh=mesh, in_specs=in_specs, out_specs=out_specs, check_vma=False)
```

```python
import functools

import jax
import jax.numpy as jnp
from jax import lax
from jax.experimental import pallas as pl
from jax.experimental.pallas import tpu as pltpu
from jax.sharding import PartitionSpec as P

epsilon = 1e-05
REACH = 3
F32 = jnp.float32
BF16 = jnp.bfloat16


def step_kernel(
    width,
    up_ref,
    own_ref,
    down_ref,
    enc_ref,
    taps_ref,
    mix_ref,
    dec_ref,
    out_ref,
    h_ref,
    v_ref,
    acc_ref,
    scale_ref,
    sum_ref,
    square_ref,
):
    halo = up_ref.shape[0]
    own = own_ref.shape[0]
    planes, _, _, lanes = h_ref.shape
    span = own_ref.shape[2]
    channels = planes * lanes
    inputs = enc_ref.shape[0]
    layers = mix_ref.shape[0]
    variables = dec_ref.shape[0]
    position = lax.axis_index("lat")
    band = position // 2
    first = band * own - halo
    height = (lax.axis_size("lat") // 2) * own
    margin = (width - span // 2) // 2
    inset = -margin % 8
    start = jnp.where(
        position % 2 == 0, span - margin - inset, span // 2 - margin - inset
    )

    def encode(source, offset):
        def one(k, _):
            y = lax.dot_general(
                source[k, :inputs],
                enc_ref[...],
                (((0,), (0,)), ((), ())),
                preferred_element_type=F32,
            )
            for chunk in range(span // 8):
                place = pl.multiple_of(8 + lax.rem(8 * chunk - start + span, span), 8)
                for t in range(planes):
                    h_ref[t, offset + k, pl.ds(place, 8), :] = y[
                        8 * chunk : 8 * chunk + 8, t * lanes : (t + 1) * lanes
                    ]
            return 0

        lax.fori_loop(0, source.shape[0], one, 0, unroll=4)

    encode(up_ref, 0)
    encode(own_ref, halo)
    encode(down_ref, halo + own)

    c0 = 2.0 * 0.7978845608028654
    c1 = 8.0 * 0.7978845608028654 * 0.044715

    for level in range(layers):
        edge = REACH * (level + 1)
        left = (inset + edge) // 8 * 8
        tiles = -(-(inset + width - edge - left) // 16)
        groups = -(-(own + 2 * halo - 2 * edge) // 4)

        def group(g, _, level=level, edge=edge, tiles=tiles, left=left + 8):
            k = 4 * g

            def convolve(j, _):
                c = pl.multiple_of(left + 16 * j, 8)
                sums = [None] * 4
                squares = [None] * 4
                for t in range(planes):
                    part = slice(t * lanes, (t + 1) * lanes)
                    rows = [h_ref[t, k + i, pl.ds(c, 16), :].astype(BF16) for i in range(10)]
                    totals = [None] * 4
                    for d in range(7):
                        tap = taps_ref[level, d, :, part]
                        for r in range(4):
                            term = rows[r + d] * tap
                            totals[r] = term if d == 0 else totals[r] + term
                    for column, d in enumerate([-3, -2, -1, 1, 2, 3]):
                        tap = taps_ref[level, 7 + column, :, part]
                        for r in range(4):
                            shifted = h_ref[t, k + r + REACH, pl.ds(c + d, 16), :].astype(BF16)
                            totals[r] = totals[r] + shifted * tap
                    for r in range(4):
                        m = pl.multiple_of(r * 16 * tiles + 16 * j, 16)
                        v_ref[pl.ds(m, 16), part] = totals[r]
                        square = totals[r] * totals[r]
                        sums[r] = totals[r] if t == 0 else sums[r] + totals[r]
                        squares[r] = square if t == 0 else squares[r] + square
                for r in range(4):
                    m = pl.multiple_of(r * 16 * tiles + 16 * j, 16)
                    sum_ref[pl.ds(m, 16), :] = sums[r].astype(F32)
                    square_ref[pl.ds(m, 16), :] = squares[r].astype(F32)
                return 0

            lax.fori_loop(0, tiles, convolve, 0)
            size = 64 * tiles
            acc_ref[:size] = jnp.dot(
                v_ref[:size], mix_ref[level], preferred_element_type=F32
            )
            for r in range(4):
                row = first + edge + k + r
                inside = jnp.logical_and(row >= 0, row < height).astype(F32)
                for j in range(tiles):
                    m = r * 16 * tiles + 16 * j
                    total = sum_ref[m : m + 16, :]
                    square = square_ref[m : m + 16, :]
                    mean = jnp.sum(total, axis=1, keepdims=True)
                    second = jnp.sum(square, axis=1, keepdims=True)
                    variance = jnp.maximum(
                        second * (1.0 / channels) - mean * mean * (1.0 / channels**2), 0.0
                    )
                    scale = lax.rsqrt(variance + epsilon) * inside
                    scale_ref[m : m + 16, :] = jnp.broadcast_to(scale, (16, lanes))
            for j in range(tiles):
                c = left + 16 * j
                for r in range(4):
                    m = r * 16 * tiles + 16 * j
                    scale = scale_ref[m : m + 16, :].astype(BF16)
                    for t in range(planes):
                        part = slice(t * lanes, (t + 1) * lanes)
                        half = acc_ref[m : m + 16, part].astype(BF16) * scale
                        inner = half * (half * half * c1 + c0)
                        gate = half + half * jnp.tanh(inner)
                        h_ref[t, k + r, c : c + 16, :] = h_ref[
                            t, k + REACH + r, c : c + 16, :
                        ] + gate.astype(F32)
            return 0

        lax.fori_loop(0, groups, group, 0)

    def decode(k, _):
        h = jnp.concatenate([h_ref[t, k, pl.ds(8, span), :] for t in range(planes)], axis=1).astype(BF16)
        y = lax.dot_general(
            dec_ref[...], h, (((1,), (1,)), ((), ())), preferred_element_type=F32
        )
        y = pltpu.roll(y, start, 1)
        out_ref[k, :variables] = (own_ref[k, :variables].astype(F32) + y).astype(BF16)
        if out_ref.shape[1] > variables:
            out_ref[k, variables:] = own_ref[k, inputs:]
        return 0

    lax.fori_loop(0, own, decode, 0, unroll=4)


def rollout_step(up, own, down, enc, taps, mix, dec, width, carry_noise):
    channels = mix.shape[1]
    variables = dec.shape[0]
    rows, lanes = own.shape[0], own.shape[2]
    total = rows + 2 * up.shape[0] + 4
    cells = 64 * (-(-(width - 2 * REACH) // 16))
    out_channels = enc.shape[0] if carry_noise else variables
    return pl.pallas_call(
        functools.partial(step_kernel, width),
        out_shape=jax.ShapeDtypeStruct((rows, out_channels, lanes), BF16),
        in_specs=[pl.BlockSpec(memory_space=pltpu.VMEM)] * 7,
        out_specs=pl.BlockSpec(memory_space=pltpu.VMEM),
        scratch_shapes=[
            pltpu.VMEM((channels // lanes, total, lanes + 24, lanes), F32),
            pltpu.VMEM((cells, channels), BF16),
            pltpu.VMEM((cells, channels), F32),
            pltpu.VMEM((cells, lanes), F32),
            pltpu.VMEM((cells, lanes), F32),
            pltpu.VMEM((cells, lanes), F32),
        ],
        compiler_params=pltpu.CompilerParams(vmem_limit_bytes=48 * 1024 * 1024),
        name="rollout_step",
    )(up, own, down, enc, taps, mix, dec)


def z_shift(block, reach, bands):
    pairs = [(i, i + reach) for i in range(bands) if 0 <= i + reach < bands]
    return lax.ppermute(block, "lat", pairs)


def local(
    state, noise, target, encoder_state_weight, enc_noise, lat_taps, lon_taps, gains, mix, decode
):
    variables, rows_dev, cols_dev = state.shape
    layers, channels = mix.shape[0], mix.shape[1]
    noise_count = noise.shape[2]
    inputs = variables + noise_count
    bands = lax.axis_size("lat")
    halo = REACH * layers
    side = 2 * halo
    core = lax.axis_index("lat") % 2
    sibling = [(i, i ^ 1) for i in range(bands)]

    gathered = jnp.concatenate([state, noise[0, 0], noise[0, 1]], axis=0)
    mine = jnp.transpose(gathered, (1, 0, 2))
    other = lax.ppermute(mine, "lat", sibling)
    low = jnp.where(core == 0, mine, other)
    high = jnp.where(core == 0, other, mine)
    block = jnp.concatenate([low, high], axis=0)
    rows = block.shape[0]
    right = block[:, :, cols_dev - side :]
    left = block[:, :, :side]
    edge = jnp.where(core == 0, right, left).reshape(4, rows // 4, -1, side)
    packed = jnp.concatenate([edge[i] for i in range(4)], axis=-1)
    mix, gains, _ = lax.optimization_barrier((mix, gains, packed))
    packed = lax.ppermute(packed, "lon", [(0, 1), (1, 0)])
    edge = jnp.concatenate([packed[:, :, i * side : (i + 1) * side] for i in range(4)], axis=0)
    block = jnp.concatenate(
        [
            jnp.where(core == 1, edge, left),
            block[:, :, side : cols_dev - side],
            jnp.where(core == 0, edge, right),
        ],
        axis=-1,
    )
    up = z_shift(block[rows - halo :, :inputs], 2, bands)
    down = z_shift(block[:halo, :inputs], -2, bands)

    enc = jnp.concatenate([encoder_state_weight, enc_noise], axis=1).T
    taps = jnp.concatenate([lat_taps, lon_taps], axis=1).astype(BF16)
    taps = jnp.broadcast_to(taps[:, :, None, :], taps.shape[:2] + (16, channels))
    scaled = mix.astype(F32) * (0.5 * gains[:, None, :])
    scaled = (scaled - jnp.mean(scaled, axis=2, keepdims=True)).astype(BF16)
    scaled = jnp.transpose(scaled, (0, 2, 1))

    first = rollout_step(up, block, down, enc, taps, scaled, decode, cols_dev // 2 + 2 * side, True)
    up = z_shift(first[rows - halo :], 2, bands)
    down = z_shift(first[:halo], -2, bands)
    second = rollout_step(up, first, down, enc, taps, scaled, decode, cols_dev // 2 + side, False)

    both = jnp.stack([first[:, :variables], second])
    lower = both[:, :rows_dev]
    upper = both[:, rows_dev:]
    kept = jnp.where(core == 0, lower, upper)
    sent = jnp.where(core == 0, upper, lower)
    taken = lax.ppermute(sent, "lat", sibling)
    lane = lax.broadcasted_iota(jnp.int32, kept.shape, 3)
    keep = (lane >= cols_dev // 2) == (core == 1)
    merged = jnp.where(keep, kept, taken)
    trajectory_predictions = jnp.transpose(merged, (0, 2, 1, 3))[None]

    members = lax.axis_size("member")
    scale = float(members)
    regrouped = lax.all_to_all(
        trajectory_predictions, "member", split_axis=2, concat_axis=0, tiled=True
    )
    quantities_real = regrouped.astype(F32)
    part = variables // members
    start = lax.axis_index("member") * part
    target_block = lax.dynamic_slice_in_dim(target, start, part, 1).astype(F32)
    skill = jnp.sum(jnp.abs(quantities_real - target_block[None]), axis=(0, 1))
    spread = jnp.zeros(skill.shape, F32)
    for i in range(members):
        for j in range(i):
            spread = spread + jnp.sum(jnp.abs(quantities_real[i] - quantities_real[j]), axis=0)
    probabilistic_error = skill / scale - spread / (scale * (scale - 1.0))
    return (trajectory_predictions, probabilistic_error)


def solution(mesh):
    in_specs = (
        P(None, "lat", "lon"),
        P("member", None, None, "lat", "lon"),
        P(None, None, "lat", "lon"),
        P(),
        P(),
        P(),
        P(),
        P(),
        P(),
        P(),
    )
    out_specs = (P("member", None, None, "lat", "lon"), P("member", "lat", "lon"))
    return jax.shard_map(local, mesh=mesh, in_specs=in_specs, out_specs=out_specs, check_vma=False)
```

```python
import functools

import jax
import jax.numpy as jnp
from jax import lax
from jax.experimental import pallas as pl
from jax.experimental.pallas import tpu as pltpu
from jax.sharding import PartitionSpec as P

epsilon = 1e-05
REACH = 3
F32 = jnp.float32
BF16 = jnp.bfloat16


def step_kernel(
    width,
    up_ref,
    own_ref,
    down_ref,
    enc_ref,
    taps_ref,
    mix_ref,
    dec_ref,
    out_ref,
    h_ref,
    v_ref,
    acc_ref,
    scale_ref,
    sum_ref,
    square_ref,
):
    halo = up_ref.shape[0]
    own = own_ref.shape[0]
    planes, _, _, lanes = h_ref.shape
    span = own_ref.shape[2]
    channels = planes * lanes
    inputs = enc_ref.shape[0]
    layers = mix_ref.shape[0]
    variables = dec_ref.shape[0]
    position = lax.axis_index("lat")
    band = position // 2
    first = band * own - halo
    height = (lax.axis_size("lat") // 2) * own
    margin = (width - span // 2) // 2
    inset = -margin % 8
    start = jnp.where(
        position % 2 == 0, span - margin - inset, span // 2 - margin - inset
    )

    def encode(source, offset):
        def one(k, _):
            y = lax.dot_general(
                source[k, :inputs],
                enc_ref[...],
                (((0,), (0,)), ((), ())),
                preferred_element_type=F32,
            )
            for chunk in range(span // 8):
                place = pl.multiple_of(8 + lax.rem(8 * chunk - start + span, span), 8)
                for t in range(planes):
                    h_ref[t, offset + k, pl.ds(place, 8), :] = y[
                        8 * chunk : 8 * chunk + 8, t * lanes : (t + 1) * lanes
                    ]
            return 0

        lax.fori_loop(0, source.shape[0], one, 0, unroll=4)

    encode(up_ref, 0)
    encode(own_ref, halo)
    encode(down_ref, halo + own)

    c0 = 2.0 * 0.7978845608028654
    c1 = 8.0 * 0.7978845608028654 * 0.044715

    for level in range(layers):
        edge = REACH * (level + 1)
        left = (inset + edge) // 8 * 8
        tiles = -(-(inset + width - edge - left) // 16)
        out_rows = own + 2 * halo - 2 * edge

        def group(g, _, level=level, edge=edge, tiles=tiles, left=left + 8, deep=4):
            k = 4 * g

            def convolve(j, _):
                c = pl.multiple_of(left + 16 * j, 8)
                sums = [None] * deep
                squares = [None] * deep
                for t in range(planes):
                    part = slice(t * lanes, (t + 1) * lanes)
                    rows = [h_ref[t, k + i, pl.ds(c, 16), :].astype(BF16) for i in range(deep + 6)]
                    totals = [None] * deep
                    for d in range(7):
                        tap = taps_ref[level, d, :, part]
                        for r in range(deep):
                            term = rows[r + d] * tap
                            totals[r] = term if d == 0 else totals[r] + term
                    for column, d in enumerate([-3, -2, -1, 1, 2, 3]):
                        tap = taps_ref[level, 7 + column, :, part]
                        for r in range(deep):
                            shifted = h_ref[t, k + r + REACH, pl.ds(c + d, 16), :].astype(BF16)
                            totals[r] = totals[r] + shifted * tap
                    for r in range(deep):
                        m = pl.multiple_of(r * 16 * tiles + 16 * j, 16)
                        v_ref[pl.ds(m, 16), part] = totals[r]
                        square = totals[r] * totals[r]
                        sums[r] = totals[r] if t == 0 else sums[r] + totals[r]
                        squares[r] = square if t == 0 else squares[r] + square
                for r in range(deep):
                    m = pl.multiple_of(r * 16 * tiles + 16 * j, 16)
                    sum_ref[pl.ds(m, 16), :] = sums[r].astype(F32)
                    square_ref[pl.ds(m, 16), :] = squares[r].astype(F32)
                return 0

            lax.fori_loop(0, tiles, convolve, 0)
            size = deep * 16 * tiles
            acc_ref[:size] = jnp.dot(
                v_ref[:size], mix_ref[level], preferred_element_type=F32
            )
            for r in range(deep):
                row = first + edge + k + r
                inside = jnp.logical_and(row >= 0, row < height).astype(F32)
                for j in range(tiles):
                    m = r * 16 * tiles + 16 * j
                    total = sum_ref[m : m + 16, :]
                    square = square_ref[m : m + 16, :]
                    mean = jnp.sum(total, axis=1, keepdims=True)
                    second = jnp.sum(square, axis=1, keepdims=True)
                    variance = jnp.maximum(
                        second * (1.0 / channels) - mean * mean * (1.0 / channels**2), 0.0
                    )
                    scale = lax.rsqrt(variance + epsilon) * inside
                    scale_ref[m : m + 16, :] = jnp.broadcast_to(scale, (16, lanes))
            for j in range(tiles):
                c = left + 16 * j
                for r in range(deep):
                    m = r * 16 * tiles + 16 * j
                    scale = scale_ref[m : m + 16, :].astype(BF16)
                    for t in range(planes):
                        part = slice(t * lanes, (t + 1) * lanes)
                        half = acc_ref[m : m + 16, part].astype(BF16) * scale
                        inner = half * (half * half * c1 + c0)
                        gate = half + half * jnp.tanh(inner)
                        h_ref[t, k + r, c : c + 16, :] = h_ref[
                            t, k + REACH + r, c : c + 16, :
                        ] + gate.astype(F32)
            return 0

        lax.fori_loop(0, out_rows // 4, group, 0)
        if out_rows % 4:
            group(out_rows // 4, 0, deep=out_rows % 4)

    def decode(k, _):
        h = jnp.concatenate([h_ref[t, k, pl.ds(8, span), :] for t in range(planes)], axis=1).astype(BF16)
        y = lax.dot_general(
            dec_ref[...], h, (((1,), (1,)), ((), ())), preferred_element_type=F32
        )
        y = pltpu.roll(y, start, 1)
        out_ref[k, :variables] = (own_ref[k, :variables].astype(F32) + y).astype(BF16)
        if out_ref.shape[1] > variables:
            out_ref[k, variables:] = own_ref[k, inputs:]
        return 0

    lax.fori_loop(0, own, decode, 0, unroll=4)


def rollout_step(up, own, down, enc, taps, mix, dec, width, carry_noise):
    channels = mix.shape[1]
    variables = dec.shape[0]
    rows, lanes = own.shape[0], own.shape[2]
    total = rows + 2 * up.shape[0] + 4
    cells = 64 * (-(-(width - 2 * REACH) // 16))
    out_channels = enc.shape[0] if carry_noise else variables
    return pl.pallas_call(
        functools.partial(step_kernel, width),
        out_shape=jax.ShapeDtypeStruct((rows, out_channels, lanes), BF16),
        in_specs=[pl.BlockSpec(memory_space=pltpu.VMEM)] * 7,
        out_specs=pl.BlockSpec(memory_space=pltpu.VMEM),
        scratch_shapes=[
            pltpu.VMEM((channels // lanes, total, lanes + 24, lanes), F32),
            pltpu.VMEM((cells, channels), BF16),
            pltpu.VMEM((cells, channels), F32),
            pltpu.VMEM((cells, lanes), F32),
            pltpu.VMEM((cells, lanes), F32),
            pltpu.VMEM((cells, lanes), F32),
        ],
        compiler_params=pltpu.CompilerParams(vmem_limit_bytes=48 * 1024 * 1024),
        name="rollout_step",
    )(up, own, down, enc, taps, mix, dec)


def z_shift(block, reach, bands):
    pairs = [(i, i + reach) for i in range(bands) if 0 <= i + reach < bands]
    return lax.ppermute(block, "lat", pairs)


def local(
    state, noise, target, encoder_state_weight, enc_noise, lat_taps, lon_taps, gains, mix, decode
):
    variables, rows_dev, cols_dev = state.shape
    layers, channels = mix.shape[0], mix.shape[1]
    noise_count = noise.shape[2]
    inputs = variables + noise_count
    bands = lax.axis_size("lat")
    halo = REACH * layers
    side = 2 * halo
    core = lax.axis_index("lat") % 2
    sibling = [(i, i ^ 1) for i in range(bands)]

    gathered = jnp.concatenate([state, noise[0, 0], noise[0, 1]], axis=0)
    mine = jnp.transpose(gathered, (1, 0, 2))
    other = lax.ppermute(mine, "lat", sibling)
    low = jnp.where(core == 0, mine, other)
    high = jnp.where(core == 0, other, mine)
    block = jnp.concatenate([low, high], axis=0)
    rows = block.shape[0]
    right = block[:, :, cols_dev - side :]
    left = block[:, :, :side]
    edge = jnp.where(core == 0, right, left).reshape(4, rows // 4, -1, side)
    packed = jnp.concatenate([edge[i] for i in range(4)], axis=-1)
    mix, gains, _ = lax.optimization_barrier((mix, gains, packed))
    packed = lax.ppermute(packed, "lon", [(0, 1), (1, 0)])
    edge = jnp.concatenate([packed[:, :, i * side : (i + 1) * side] for i in range(4)], axis=0)
    block = jnp.concatenate(
        [
            jnp.where(core == 1, edge, left),
            block[:, :, side : cols_dev - side],
            jnp.where(core == 0, edge, right),
        ],
        axis=-1,
    )
    up = z_shift(block[rows - halo :, :inputs], 2, bands)
    down = z_shift(block[:halo, :inputs], -2, bands)

    encoder_state_weight, enc_noise, lat_taps, lon_taps, _ = lax.optimization_barrier(
        (encoder_state_weight, enc_noise, lat_taps, lon_taps, up)
    )
    enc = jnp.concatenate([encoder_state_weight, enc_noise], axis=1).T
    taps = jnp.concatenate([lat_taps, lon_taps], axis=1).astype(BF16)
    taps = jnp.broadcast_to(taps[:, :, None, :], taps.shape[:2] + (16, channels))
    scaled = mix.astype(F32) * (0.5 * gains[:, None, :])
    scaled = (scaled - jnp.mean(scaled, axis=2, keepdims=True)).astype(BF16)
    scaled = jnp.transpose(scaled, (0, 2, 1))

    first = rollout_step(up, block, down, enc, taps, scaled, decode, cols_dev // 2 + 2 * side, True)
    up = z_shift(first[rows - halo :], 2, bands)
    down = z_shift(first[:halo], -2, bands)
    second = rollout_step(up, first, down, enc, taps, scaled, decode, cols_dev // 2 + side, False)

    both = jnp.stack([first[:, :variables], second])
    lower = both[:, :rows_dev]
    upper = both[:, rows_dev:]
    kept = jnp.where(core == 0, lower, upper)
    sent = jnp.where(core == 0, upper, lower)
    taken = lax.ppermute(sent, "lat", sibling)
    lane = lax.broadcasted_iota(jnp.int32, kept.shape, 3)
    keep = (lane >= cols_dev // 2) == (core == 1)
    merged = jnp.where(keep, kept, taken)
    trajectory_predictions = jnp.transpose(merged, (0, 2, 1, 3))[None]

    members = lax.axis_size("member")
    scale = float(members)
    regrouped = lax.all_to_all(
        trajectory_predictions, "member", split_axis=2, concat_axis=0, tiled=True
    )
    quantities_real = regrouped.astype(F32)
    part = variables // members
    start = lax.axis_index("member") * part
    target_block = lax.dynamic_slice_in_dim(target, start, part, 1).astype(F32)
    skill = jnp.sum(jnp.abs(quantities_real - target_block[None]), axis=(0, 1))
    spread = jnp.zeros(skill.shape, F32)
    for i in range(members):
        for j in range(i):
            spread = spread + jnp.sum(jnp.abs(quantities_real[i] - quantities_real[j]), axis=0)
    probabilistic_error = skill / scale - spread / (scale * (scale - 1.0))
    return (trajectory_predictions, probabilistic_error)


def solution(mesh):
    in_specs = (
        P(None, "lat", "lon"),
        P("member", None, None, "lat", "lon"),
        P(None, None, "lat", "lon"),
        P(),
        P(),
        P(),
        P(),
        P(),
        P(),
        P(),
    )
    out_specs = (P("member", None, None, "lat", "lon"), P("member", "lat", "lon"))
    return jax.shard_map(local, mesh=mesh, in_specs=in_specs, out_specs=out_specs, check_vma=False)
```

```python
import functools

import jax
import jax.numpy as jnp
from jax import lax
from jax.experimental import pallas as pl
from jax.experimental.pallas import tpu as pltpu
from jax.sharding import PartitionSpec as P

epsilon = 1e-05
REACH = 3
F32 = jnp.float32
BF16 = jnp.bfloat16


def step_kernel(
    width,
    up_ref,
    own_ref,
    down_ref,
    enc_ref,
    taps_ref,
    mix_ref,
    dec_ref,
    out_ref,
    h_ref,
    v_ref,
    acc_ref,
    scale_ref,
    sum_ref,
    square_ref,
):
    halo = up_ref.shape[0]
    own = own_ref.shape[0]
    planes, _, _, lanes = h_ref.shape
    span = own_ref.shape[2]
    channels = planes * lanes
    inputs = enc_ref.shape[0]
    layers = mix_ref.shape[0]
    variables = dec_ref.shape[0]
    position = lax.axis_index("lat")
    band = position // 2
    first = band * own - halo
    height = (lax.axis_size("lat") // 2) * own
    margin = (width - span // 2) // 2
    inset = -margin % 8
    start = jnp.where(
        position % 2 == 0, span - margin - inset, span // 2 - margin - inset
    )

    def encode(source, offset):
        def one(k, _):
            y = lax.dot_general(
                source[k, :inputs],
                enc_ref[...],
                (((0,), (0,)), ((), ())),
                preferred_element_type=F32,
            )
            for chunk in range(span // 8):
                place = pl.multiple_of(8 + lax.rem(8 * chunk - start + span, span), 8)
                for t in range(planes):
                    h_ref[t, offset + k, pl.ds(place, 8), :] = y[
                        8 * chunk : 8 * chunk + 8, t * lanes : (t + 1) * lanes
                    ]
            return 0

        lax.fori_loop(0, source.shape[0], one, 0, unroll=4)

    encode(up_ref, 0)
    encode(own_ref, halo)
    encode(down_ref, halo + own)

    c0 = 2.0 * 0.7978845608028654
    c1 = 8.0 * 0.7978845608028654 * 0.044715

    for level in range(layers):
        edge = REACH * (level + 1)
        left = (inset + edge) // 8 * 8
        tiles = -(-(inset + width - edge - left) // 16)
        out_rows = own + 2 * halo - 2 * edge

        def group(g, _, level=level, edge=edge, tiles=tiles, left=left + 8, deep=8):
            k = 8 * g

            def convolve(j, _):
                c = pl.multiple_of(left + 16 * j, 8)
                sums = [None] * deep
                squares = [None] * deep
                for t in range(planes):
                    part = slice(t * lanes, (t + 1) * lanes)
                    rows = [h_ref[t, k + i, pl.ds(c, 16), :].astype(BF16) for i in range(deep + 6)]
                    totals = [None] * deep
                    for d in range(7):
                        tap = taps_ref[level, d, :, part]
                        for r in range(deep):
                            term = rows[r + d] * tap
                            totals[r] = term if d == 0 else totals[r] + term
                    for column, d in enumerate([-3, -2, -1, 1, 2, 3]):
                        tap = taps_ref[level, 7 + column, :, part]
                        for r in range(deep):
                            shifted = h_ref[t, k + r + REACH, pl.ds(c + d, 16), :].astype(BF16)
                            totals[r] = totals[r] + shifted * tap
                    for r in range(deep):
                        m = pl.multiple_of(r * 16 * tiles + 16 * j, 16)
                        v_ref[pl.ds(m, 16), part] = totals[r]
                        square = totals[r] * totals[r]
                        sums[r] = totals[r] if t == 0 else sums[r] + totals[r]
                        squares[r] = square if t == 0 else squares[r] + square
                for r in range(deep):
                    m = pl.multiple_of(r * 16 * tiles + 16 * j, 16)
                    sum_ref[pl.ds(m, 16), :] = sums[r].astype(F32)
                    square_ref[pl.ds(m, 16), :] = squares[r].astype(F32)
                return 0

            lax.fori_loop(0, tiles, convolve, 0)
            size = deep * 16 * tiles
            acc_ref[:size] = jnp.dot(
                v_ref[:size], mix_ref[level], preferred_element_type=F32
            )
            for r in range(deep):
                row = first + edge + k + r
                inside = jnp.logical_and(row >= 0, row < height).astype(F32)
                for j in range(tiles):
                    m = r * 16 * tiles + 16 * j
                    total = sum_ref[m : m + 16, :]
                    square = square_ref[m : m + 16, :]
                    mean = jnp.sum(total, axis=1, keepdims=True)
                    second = jnp.sum(square, axis=1, keepdims=True)
                    variance = jnp.maximum(
                        second * (1.0 / channels) - mean * mean * (1.0 / channels**2), 0.0
                    )
                    scale = lax.rsqrt(variance + epsilon) * inside
                    scale_ref[m : m + 16, :] = jnp.broadcast_to(scale, (16, lanes))
            for j in range(tiles):
                c = left + 16 * j
                for r in range(deep):
                    m = r * 16 * tiles + 16 * j
                    scale = scale_ref[m : m + 16, :].astype(BF16)
                    for t in range(planes):
                        part = slice(t * lanes, (t + 1) * lanes)
                        half = acc_ref[m : m + 16, part].astype(BF16) * scale
                        inner = half * (half * half * c1 + c0)
                        gate = half + half * jnp.tanh(inner)
                        h_ref[t, k + r, c : c + 16, :] = h_ref[
                            t, k + REACH + r, c : c + 16, :
                        ] + gate.astype(F32)
            return 0

        lax.fori_loop(0, out_rows // 8, group, 0)
        if out_rows % 8:
            group(out_rows // 8, 0, deep=out_rows % 8)

    def decode(k, _):
        h = jnp.concatenate([h_ref[t, k, pl.ds(8, span), :] for t in range(planes)], axis=1).astype(BF16)
        y = lax.dot_general(
            dec_ref[...], h, (((1,), (1,)), ((), ())), preferred_element_type=F32
        )
        y = pltpu.roll(y, start, 1)
        out_ref[k, :variables] = (own_ref[k, :variables].astype(F32) + y).astype(BF16)
        if out_ref.shape[1] > variables:
            out_ref[k, variables:] = own_ref[k, inputs:]
        return 0

    lax.fori_loop(0, own, decode, 0, unroll=4)


def rollout_step(up, own, down, enc, taps, mix, dec, width, carry_noise):
    channels = mix.shape[1]
    variables = dec.shape[0]
    rows, lanes = own.shape[0], own.shape[2]
    total = rows + 2 * up.shape[0] + 4
    cells = 128 * (-(-(width - 2 * REACH) // 16))
    out_channels = enc.shape[0] if carry_noise else variables
    return pl.pallas_call(
        functools.partial(step_kernel, width),
        out_shape=jax.ShapeDtypeStruct((rows, out_channels, lanes), BF16),
        in_specs=[pl.BlockSpec(memory_space=pltpu.VMEM)] * 7,
        out_specs=pl.BlockSpec(memory_space=pltpu.VMEM),
        scratch_shapes=[
            pltpu.VMEM((channels // lanes, total, lanes + 24, lanes), F32),
            pltpu.VMEM((cells, channels), BF16),
            pltpu.VMEM((cells, channels), F32),
            pltpu.VMEM((cells, lanes), F32),
            pltpu.VMEM((cells, lanes), F32),
            pltpu.VMEM((cells, lanes), F32),
        ],
        compiler_params=pltpu.CompilerParams(vmem_limit_bytes=48 * 1024 * 1024),
        name="rollout_step",
    )(up, own, down, enc, taps, mix, dec)


def z_shift(block, reach, bands):
    pairs = [(i, i + reach) for i in range(bands) if 0 <= i + reach < bands]
    return lax.ppermute(block, "lat", pairs)


def local(
    state, noise, target, encoder_state_weight, enc_noise, lat_taps, lon_taps, gains, mix, decode
):
    variables, rows_dev, cols_dev = state.shape
    layers, channels = mix.shape[0], mix.shape[1]
    noise_count = noise.shape[2]
    inputs = variables + noise_count
    bands = lax.axis_size("lat")
    halo = REACH * layers
    side = 2 * halo
    core = lax.axis_index("lat") % 2
    sibling = [(i, i ^ 1) for i in range(bands)]

    gathered = jnp.concatenate([state, noise[0, 0], noise[0, 1]], axis=0)
    mine = jnp.transpose(gathered, (1, 0, 2))
    other = lax.ppermute(mine, "lat", sibling)
    low = jnp.where(core == 0, mine, other)
    high = jnp.where(core == 0, other, mine)
    block = jnp.concatenate([low, high], axis=0)
    rows = block.shape[0]
    right = block[:, :, cols_dev - side :]
    left = block[:, :, :side]
    edge = jnp.where(core == 0, right, left).reshape(4, rows // 4, -1, side)
    packed = jnp.concatenate([edge[i] for i in range(4)], axis=-1)
    mix, gains, _ = lax.optimization_barrier((mix, gains, packed))
    packed = lax.ppermute(packed, "lon", [(0, 1), (1, 0)])
    edge = jnp.concatenate([packed[:, :, i * side : (i + 1) * side] for i in range(4)], axis=0)
    block = jnp.concatenate(
        [
            jnp.where(core == 1, edge, left),
            block[:, :, side : cols_dev - side],
            jnp.where(core == 0, edge, right),
        ],
        axis=-1,
    )
    up = z_shift(block[rows - halo :, :inputs], 2, bands)
    down = z_shift(block[:halo, :inputs], -2, bands)

    encoder_state_weight, enc_noise, lat_taps, lon_taps, _ = lax.optimization_barrier(
        (encoder_state_weight, enc_noise, lat_taps, lon_taps, up)
    )
    enc = jnp.concatenate([encoder_state_weight, enc_noise], axis=1).T
    taps = jnp.concatenate([lat_taps, lon_taps], axis=1).astype(BF16)
    taps = jnp.broadcast_to(taps[:, :, None, :], taps.shape[:2] + (16, channels))
    scaled = mix.astype(F32) * (0.5 * gains[:, None, :])
    scaled = (scaled - jnp.mean(scaled, axis=2, keepdims=True)).astype(BF16)
    scaled = jnp.transpose(scaled, (0, 2, 1))

    first = rollout_step(up, block, down, enc, taps, scaled, decode, cols_dev // 2 + 2 * side, True)
    up = z_shift(first[rows - halo :], 2, bands)
    down = z_shift(first[:halo], -2, bands)
    second = rollout_step(up, first, down, enc, taps, scaled, decode, cols_dev // 2 + side, False)

    both = jnp.stack([first[:, :variables], second])
    lower = both[:, :rows_dev]
    upper = both[:, rows_dev:]
    kept = jnp.where(core == 0, lower, upper)
    sent = jnp.where(core == 0, upper, lower)
    taken = lax.ppermute(sent, "lat", sibling)
    lane = lax.broadcasted_iota(jnp.int32, kept.shape, 3)
    keep = (lane >= cols_dev // 2) == (core == 1)
    merged = jnp.where(keep, kept, taken)
    trajectory_predictions = jnp.transpose(merged, (0, 2, 1, 3))[None]

    members = lax.axis_size("member")
    scale = float(members)
    regrouped = lax.all_to_all(
        trajectory_predictions, "member", split_axis=2, concat_axis=0, tiled=True
    )
    quantities_real = regrouped.astype(F32)
    part = variables // members
    start = lax.axis_index("member") * part
    target_block = lax.dynamic_slice_in_dim(target, start, part, 1).astype(F32)
    skill = jnp.sum(jnp.abs(quantities_real - target_block[None]), axis=(0, 1))
    spread = jnp.zeros(skill.shape, F32)
    for i in range(members):
        for j in range(i):
            spread = spread + jnp.sum(jnp.abs(quantities_real[i] - quantities_real[j]), axis=0)
    probabilistic_error = skill / scale - spread / (scale * (scale - 1.0))
    return (trajectory_predictions, probabilistic_error)


def solution(mesh):
    in_specs = (
        P(None, "lat", "lon"),
        P("member", None, None, "lat", "lon"),
        P(None, None, "lat", "lon"),
        P(),
        P(),
        P(),
        P(),
        P(),
        P(),
        P(),
    )
    out_specs = (P("member", None, None, "lat", "lon"), P("member", "lat", "lon"))
    return jax.shard_map(local, mesh=mesh, in_specs=in_specs, out_specs=out_specs, check_vma=False)
```
